512 devices in a mesh: ctx: 64 (over x, z, core), head: 8 (over y).
Axes of the slice: x: 4, y: 8, z: 8, core: 2. Of those that a mesh axis runs over, the one named last changes fastest.
Arguments:
- queries: bfloat16 [16384, 4096], P('ctx', 'head'), may hold values from -180 to 180
- keys: bfloat16 [16384, 1024], P('ctx', 'head'), may hold values from -6.5 to 6.5
- values: bfloat16 [16384, 1024], P('ctx', 'head'), may hold values from -6 to 6
- out_grad: bfloat16 [16384, 4096], P('ctx', 'head'), may hold values from -6 to 6
- attn_out: bfloat16 [16384, 4096], P('ctx', 'head'), may hold values from -6 to 6
- lengths: int32 [64], replicated, may hold values from 1 to 1792, as said below
- proj_weight: bfloat16 [4096, 8, 768], P('ctx', 'head'), may hold values from -0.078125 to 0.078125
Outputs:
- input_grad: bfloat16 [16384, 4096], P('ctx', 'head')
The draws below stay inside these ranges and needn't reach their ends.
Inputs may be any that keep to these rules, and one draw needn't show every extreme that they name: `lengths`: every document has 1 to 1792 tokens, one has exactly 1792, and they sum to 16384.
All inputs are finite; a program needn't handle non-finite values.
Results may differ from the reference program's by a relative error of at most 0.013.
Values may be sent and summed in bfloat16 or wider, within the bound.
No kernel may reach another device: no remote copies, remote signals or barrier semaphores. Data moves between devices by JAX's collectives and lax.ppermute only.
A program may use at most 64 MiB of HBM per device.

```python
import jax
import jax.numpy as jnp
from jax import lax

D = 4096
HQ = 32
KVH = 8
HD = 128
TOK_DEV = 256
REACH = 7
TOKENS = 16384
DOCS = 64
MAXDOC = 1792
GROUP = 4
N_CTX = 64
N_HEAD = 8


def shared_draw(key):
    query_key = jax.random.fold_in(key, 11)
    keys_key = jax.random.fold_in(key, 12)
    keys = jnp.clip(jax.random.normal(keys_key, (TOKENS, KVH * HD), jnp.float32), -6.0, 6.0)
    queries = jnp.clip(jax.random.normal(query_key, (TOKENS, HQ * HD), jnp.float32), -6.0, 6.0)
    return (queries, keys)


def draw_queries(key, part):
    return shared_draw(key)[0].astype(jnp.bfloat16)


def draw_keys(key, part):
    return shared_draw(key)[1].astype(jnp.bfloat16)


def draw_lengths(key, part):
    jitter_key = jax.random.fold_in(key, 21)
    tail_len = TOK_DEV // 2
    front_total = TOKENS - MAXDOC - tail_len
    front_docs = DOCS - 2
    spacing = front_total // front_docs
    steps = jnp.arange(1, front_docs, dtype=jnp.int32)
    jitter = jax.random.randint(jitter_key, (front_docs - 1,), 0, spacing // 2 + 1, jnp.int32)
    cuts = steps * spacing + jitter
    bounds = jnp.concatenate([jnp.zeros((1,), jnp.int32), cuts, jnp.full((1,), front_total, jnp.int32)])
    front = (bounds[1:] - bounds[:-1]).astype(jnp.int32)
    return jnp.concatenate([front, jnp.full((1,), MAXDOC, jnp.int32), jnp.full((1,), tail_len, jnp.int32)]).astype(jnp.int32)


def block_levels(own_key, extent, split, smallest, largest):
    factor_of, own = 1.0, jax.random.fold_in(own_key, 6)
    for dim, blocks in split:
        steps = jnp.exp(jax.random.uniform(jax.random.fold_in(own, dim), (blocks,), jnp.float32, smallest / len(split), largest / len(split)))
        factor_of = factor_of * jnp.repeat(steps, extent[dim] // blocks).reshape([-1 if axis == dim else 1 for axis in range(len(extent))])
    return factor_of


def scatter_about(key, extent, scale, limit, pieces=(), kind=jnp.bfloat16):
    entries = jax.random.normal(key, extent, jnp.float32) * scale
    if len(pieces) > 0:
        entries = block_levels(key, extent, pieces, -0.22, 0.18) * entries
    return jnp.clip(entries, min=-limit, max=limit).astype(kind)


def setup_inputs(seed: int = 0) -> dict:
    seeds = jax.random.split(jax.random.key(seed), 8)
    return {
        "queries": draw_queries(jax.random.fold_in(seeds[7], 71), 0),
        "keys": draw_keys(jax.random.fold_in(seeds[7], 71), 0),
        "values": scatter_about(seeds[2], (TOKENS, KVH * HD), 1.0, 6.0, ((0, 64), (1, 8))),
        "out_grad": scatter_about(seeds[3], (TOKENS, HQ * HD), 1.0, 6.0, ((0, 64), (1, 8))),
        "attn_out": scatter_about(seeds[4], (TOKENS, HQ * HD), 1.0, 6.0, ((0, 64), (1, 8))),
        "lengths": draw_lengths(jax.random.fold_in(seeds[7], 71), 0),
        "proj_weight": scatter_about(seeds[6], (D, KVH, (GROUP + 2) * HD), ((HQ + 2 * KVH) * HD) ** -0.5, 0.078125, ((0, 64), (1, 8))),
    }


def doc_number(positions, ends):
    counted = jnp.sum((positions[:, None] >= ends[None, :]).astype(jnp.int32), axis=1)
    return jnp.where(positions >= 0, counted, -1).astype(jnp.int32)


def reference(queries, keys, values, out_grad, attn_out, lengths, proj_weight):
    group = HQ // KVH
    window = (REACH + 1) * TOK_DEV
    margin = REACH * TOK_DEV
    scale_factor = HD ** -0.5
    ends = jnp.cumsum(lengths).astype(jnp.int32)
    delta_all = jnp.sum(
        (out_grad.astype(jnp.float32) * attn_out.astype(jnp.float32)).reshape(TOKENS, KVH, group, HD), axis=3)
    key_pad = jnp.concatenate([jnp.zeros((margin, KVH, HD), jnp.float32),
                               keys.astype(jnp.float32).reshape(TOKENS, KVH, HD)], axis=0)
    value_pad = jnp.concatenate([jnp.zeros((margin, KVH, HD), jnp.float32),
                                 values.astype(jnp.float32).reshape(TOKENS, KVH, HD)], axis=0)
    query_all = queries.astype(jnp.float32).reshape(TOKENS, KVH, group, HD)
    dout_all = out_grad.astype(jnp.float32).reshape(TOKENS, KVH, group, HD)

    def one_tile(carry, tile_index):
        key_acc, value_acc = carry
        first = (tile_index * TOK_DEV).astype(jnp.int32)
        query_tile = lax.dynamic_slice_in_dim(query_all, first, TOK_DEV, 0)
        dout_tile = lax.dynamic_slice_in_dim(dout_all, first, TOK_DEV, 0)
        delta_tile = lax.dynamic_slice_in_dim(delta_all, first, TOK_DEV, 0)
        key_tile = lax.dynamic_slice_in_dim(key_pad, first, window, 0)
        value_tile = lax.dynamic_slice_in_dim(value_pad, first, window, 0)
        query_pos = first + jnp.arange(TOK_DEV, dtype=jnp.int32)
        key_pos = first - margin + jnp.arange(window, dtype=jnp.int32)
        allowed = (doc_number(query_pos, ends)[:, None] == doc_number(key_pos, ends)[None, :]) & (
            key_pos[None, :] <= query_pos[:, None])
        scores = jnp.einsum('tkgd,ukd->kgtu', query_tile, key_tile) * scale_factor
        row_max = jnp.max(jnp.where(allowed[None, None], scores, -1e30), axis=3, keepdims=True)
        total = jnp.sum(jnp.where(allowed[None, None], jnp.exp(scores - row_max), 0.0), axis=3, keepdims=True)
        lse_tile = row_max + jnp.log(total)
        probs = jnp.where(allowed[None, None], jnp.exp(scores - lse_tile), 0.0)
        probs_low = lax.optimization_barrier(probs.astype(jnp.bfloat16)).astype(jnp.float32)
        value_grad = jnp.einsum('kgtu,tkgd->ukd', probs_low, dout_tile)
        dprobs = jnp.einsum('tkgd,ukd->kgtu', dout_tile, value_tile)
        delta_here = jnp.transpose(delta_tile, (1, 2, 0))[..., None]
        dscore = (probs * (dprobs - delta_here) * scale_factor).astype(jnp.bfloat16)
        dscore = lax.optimization_barrier(dscore).astype(jnp.float32)
        query_grad = jnp.einsum('kgtu,ukd->tkgd', dscore, key_tile).astype(jnp.bfloat16)
        key_grad = jnp.einsum('kgtu,tkgd->ukd', dscore, query_tile)
        old_keys = lax.dynamic_slice_in_dim(key_acc, first, window, 0)
        old_values = lax.dynamic_slice_in_dim(value_acc, first, window, 0)
        key_acc = lax.dynamic_update_slice_in_dim(key_acc, old_keys + key_grad, first, 0)
        value_acc = lax.dynamic_update_slice_in_dim(value_acc, old_values + value_grad, first, 0)
        return (key_acc, value_acc), query_grad

    start_acc = jnp.zeros((TOKENS + margin, KVH, HD), jnp.float32)
    (key_acc, value_acc), query_tiles = lax.scan(one_tile, (start_acc, start_acc),
                                                 jnp.arange(N_CTX, dtype=jnp.int32))
    query_grad = query_tiles.reshape(TOKENS, KVH, group * HD)
    key_grad = key_acc[margin:].astype(jnp.bfloat16)
    value_grad = value_acc[margin:].astype(jnp.bfloat16)
    combined = jnp.concatenate([query_grad, key_grad, value_grad], axis=2)
    per_block = KVH // N_HEAD
    total = jnp.zeros((TOKENS, D), jnp.float32)
    for block in range(N_HEAD):
        cols = combined[:, block * per_block:(block + 1) * per_block].reshape(TOKENS, -1)
        weights = proj_weight[:, block * per_block:(block + 1) * per_block].reshape(D, -1)
        block_part = lax.dot_general(cols, weights, (((1,), (1,)), ((), ())),
                                     preferred_element_type=jnp.float32).astype(jnp.bfloat16)
        total = total + lax.optimization_barrier(block_part).astype(jnp.float32)
    return total.astype(jnp.bfloat16)
```

```python
import functools

import jax
import jax.numpy as jnp
from jax import lax
from jax.experimental import pallas as pl
from jax.experimental.pallas import tpu as pltpu
from jax.sharding import PartitionSpec as P

HD = 128
GROUP = 4
TILE = 256
NX = 4
NZ = 8
NCHIP = NX * NZ
NHEAD = 8
SLOTS = 8
Z_ORDER = (0, 4, 2, 6, 1, 5, 3, 7)
LOG2E = 1.4426950408889634
SCALE = HD ** (-0.5)
F32 = jnp.float32
BF16 = jnp.bfloat16


def chip_shift(by):
    return [(2 * q + c, 2 * ((q + by) % NCHIP) + c) for q in range(NCHIP) for c in range(2)]


def z_shift(by):
    return [
        (2 * (NZ * x + z) + c, 2 * (NZ * x + (z + by) % NZ) + c)
        for x in range(NX) for z in range(NZ) for c in range(2)
    ]


def x_shift(by):
    return [
        (2 * (NZ * x + z) + c, 2 * (NZ * ((x + by) % NX) + z) + c)
        for x in range(NX) for z in range(NZ) for c in range(2)
    ]


CORE_SWAP = [(d, d ^ 1) for d in range(2 * NCHIP)]
LAST_TILE = [(2 * q, 2 * q + 1) for q in range(NCHIP)] + [
    (2 * q + 1, 2 * ((q + 4) % NCHIP)) for q in range(NCHIP)
]
LAST_TILE_BACK = [(b, a) for a, b in LAST_TILE]


def weight_transpose():
    pairs = []
    for x in range(NX):
        for z in range(NZ):
            for c in range(2):
                for a in range(NX):
                    for b in range(2):
                        src = (2 * (NZ * x + z) + c) * NHEAD + 2 * a + b
                        dst = (2 * (NZ * a + z) + c) * NHEAD + 2 * x + b
                        pairs.append((src, dst))
    return pairs


def head_shift(by):
    return [(j, (j + by) % NHEAD) for j in range(NHEAD)]


HEAD_PAIR = [(j, j ^ 1) for j in range(NHEAD)]

NT = (((1,), (1,)), ((), ()))
NN = (((1,), (0,)), ((), ()))
TN = (((0,), (0,)), ((), ()))


def dot(a, b, dims):
    return lax.dot_general(a, b, dims, preferred_element_type=F32)


def attention_kernel(
    base, start_ref, delta_ref, q_ref, do_ref, own, last, o1, o23, x123,
    dq_ref, g_own, g_last, g_x, scores,
):
    own_base = base[0]
    q_all = jnp.concatenate([q_ref[:, h * HD:(h + 1) * HD] for h in range(GROUP)], axis=0)
    do_all = jnp.concatenate([do_ref[:, h * HD:(h + 1) * HD] for h in range(GROUP)], axis=0)
    start = start_ref[...]
    q_pos = own_base + lax.broadcasted_iota(jnp.int32, (1, TILE), 1)
    row = lax.broadcasted_iota(jnp.int32, (TILE, TILE), 0)
    tiles = [own, o1, o23.at[0], o23.at[1], last, x123.at[0], x123.at[1], x123.at[2]]
    width = GROUP * TILE
    top = jnp.full((8, width), -1e30, F32)
    for t, tile in enumerate(tiles):
        raw = dot(tile[:, :HD], q_all, NT)
        k_pos = base[t] + row
        allowed = (k_pos >= start) & (k_pos <= q_pos)
        parts = []
        for h in range(GROUP):
            part = jnp.where(allowed, raw[:, h * TILE:(h + 1) * TILE], -1e30)
            scores[pl.ds(t * TILE, TILE), pl.ds(h * TILE, TILE)] = part
            parts.append(jnp.max(part.reshape(TILE // 8, 8, TILE), axis=0))
        top = jnp.maximum(top, jnp.concatenate(parts, axis=1))
    top = jnp.max(top, axis=0, keepdims=True)
    total = jnp.zeros((8, width), F32)
    for t in range(SLOTS):
        e = jnp.exp2((scores[pl.ds(t * TILE, TILE), :] - top) * (SCALE * LOG2E))
        scores[pl.ds(t * TILE, TILE), :] = e
        total = total + jnp.sum(e.reshape(TILE // 8, 8, width), axis=0)
    total = jnp.sum(total, axis=0, keepdims=True)
    inv = 1.0 / total
    delta = delta_ref[...]
    dq = [jnp.zeros((TILE, HD), F32) for _ in range(GROUP)]
    for t, tile in enumerate(tiles):
        probs = scores[pl.ds(t * TILE, TILE), :] * inv
        dprobs = dot(tile[:, HD:], do_all, NT)
        dscore = (probs * (dprobs - delta) * SCALE).astype(BF16)
        dv = dot(probs.astype(BF16), do_all, NN)
        dk = dot(dscore, q_all, NN)
        for h in range(GROUP):
            dq[h] = dq[h] + dot(dscore[:, h * TILE:(h + 1) * TILE], tile[:, :HD], TN)
        if t < 4:
            g_own[t, :, :HD] = dk
            g_own[t, :, HD:] = dv
        elif t == 4:
            g_last[:, :HD] = dk.astype(BF16)
            g_last[:, HD:] = dv.astype(BF16)
        else:
            g_x[t - 5, :, :HD] = dk.astype(BF16)
            g_x[t - 5, :, HD:] = dv.astype(BF16)
    for h in range(GROUP):
        dq_ref[:, h * HD:(h + 1) * HD] = dq[h].astype(BF16)


def assemble_kernel(where_, *refs):
    pieces, (wq_ref, wkv_ref) = refs[:8], refs[8:]
    z, core, half, first = where_[0], where_[1], where_[2], where_[3]
    for s in range(NX):
        r = (first + s) % NX
        for side in range(2):
            c = core if side == 0 else 1 - core
            for i, step in enumerate(Z_ORDER):
                zz = (z + step) % NZ
                kept = jnp.where(zz // 4 == half, 4, 0)
                at = pl.multiple_of((kept + zz % 4) * 128 + c * 64, 64)
                piece = pieces[2 * s + side][i]
                wq_ref[r, pl.ds(at, 64), :] = piece[:, :512]
                wkv_ref[r, pl.ds(at, 64), :] = piece[:, 512:]


def proj_q_kernel(d0, d1, d2, d3, wq_ref, acc_ref):
    for n in range(2):
        cols = slice(n * 512, (n + 1) * 512)
        acc = dot(d0[...], wq_ref[0, cols, :], NT)
        for r, d in ((1, d1), (2, d2), (3, d3)):
            acc = acc + dot(d[...], wq_ref[r, cols, :], NT)
        acc_ref[:, cols] = acc


def proj_kv_kernel(d0, d1, d2, d3, wkv_ref, acc_ref, send_ref, keep_ref):
    for n in range(2):
        cols = slice(n * 512, (n + 1) * 512)
        acc = acc_ref[:, cols]
        for r, d in enumerate((d0, d1, d2, d3)):
            acc = acc + dot(d[...], wkv_ref[r, cols, :], NT)
        if n == 0:
            send_ref[...] = acc.astype(BF16)
        else:
            keep_ref[...] = acc


def call(kernel, n_scalar, args, outs, scratch=(), flops=0, nbytes=0):
    vmem = pl.BlockSpec(memory_space=pltpu.VMEM)
    smem = pl.BlockSpec(memory_space=pltpu.SMEM)
    return pl.pallas_call(
        kernel,
        out_shape=outs,
        in_specs=[smem] * n_scalar + [vmem] * (len(args) - n_scalar),
        out_specs=jax.tree.map(lambda _: vmem, outs),
        scratch_shapes=list(scratch),
        cost_estimate=pl.CostEstimate(flops=flops, bytes_accessed=nbytes, transcendentals=0),
        compiler_params=pltpu.CompilerParams(vmem_limit_bytes=48 * 1024 * 1024),
    )(*args)


def sds(shape, dtype):
    return jax.ShapeDtypeStruct(shape, dtype)


def shards(queries, keys, values, out_grad, attn_out, lengths, proj_weight):
    i = lax.axis_index("ctx")
    j = lax.axis_index("head")
    chip, core = i // 2, i % 2
    x, z = chip // NZ, chip % NZ
    k, b = j // 2, j % 2

    own = jnp.concatenate([keys, values], axis=1)
    last = lax.ppermute(own, "ctx", LAST_TILE)
    o1 = lax.ppermute(own, "ctx", chip_shift(1))
    o23 = lax.ppermute(jnp.stack([own, o1]), "ctx", chip_shift(2))
    x123 = lax.ppermute(jnp.concatenate([o1[None], o23]), "ctx", CORE_SWAP)

    w = lax.ppermute(proj_weight.reshape(64, 768), ("ctx", "head"), weight_transpose())
    w = w[None]
    for by in (4, 2, 1):
        w = jnp.concatenate([w, lax.ppermute(w, "ctx", z_shift(-by))])
    pieces = [w] + [lax.ppermute(w, "ctx", x_shift(-s)) for s in (1, 2, 3)]
    both = []
    for piece in pieces:
        both += [piece, lax.ppermute(piece, "ctx", CORE_SWAP)]
    whereabouts = jnp.stack([z, core, b, (x - k) % NX]).astype(jnp.int32)
    wq, wkv = call(
        assemble_kernel, 1, [whereabouts] + both,
        (sds((NX, 1024, 512), BF16), sds((NX, 1024, 256), BF16)), nbytes=12_000_000,
    )

    ends = jnp.cumsum(lengths)
    q_pos = i * TILE + jnp.arange(TILE, dtype=jnp.int32)
    start = jnp.max(jnp.where(ends[:, None] <= q_pos[None, :], ends[:, None], 0), axis=0, keepdims=True)
    own_tiles = [2 * (chip - n) + core for n in range(4)]
    last_tile = jnp.where(core == 1, 2 * chip, 2 * chip - 7)
    other_tiles = [2 * (chip - n) + 1 - core for n in range(1, 4)]
    base = (jnp.stack(own_tiles + [last_tile] + other_tiles) * TILE).astype(jnp.int32)
    delta = jnp.sum(
        (out_grad.astype(F32) * attn_out.astype(F32)).reshape(TILE, GROUP, HD), axis=2
    ).T.reshape(1, GROUP * TILE)

    dq, g_own, g_last, g_x = call(
        attention_kernel, 1,
        [base, start, delta, queries, out_grad, own, last, o1, o23, x123],
        (
            sds((TILE, GROUP * HD), BF16),
            sds((4, TILE, 2 * HD), F32),
            sds((TILE, 2 * HD), BF16),
            sds((3, TILE, 2 * HD), BF16),
        ),
        scratch=[pltpu.VMEM((SLOTS * TILE, GROUP * TILE), F32)],
        flops=2_700_000_000, nbytes=5_000_000,
    )

    x_back = lax.ppermute(g_x, "ctx", CORE_SWAP).astype(F32)
    last_back = lax.ppermute(g_last, "ctx", LAST_TILE_BACK)
    far = (g_own[2:] + x_back[1:]).astype(BF16)
    far_back = lax.ppermute(far, "ctx", chip_shift(-2)).astype(F32)
    near = (g_own[1] + x_back[0] + far_back[1]).astype(BF16)
    near_back = lax.ppermute(near, "ctx", chip_shift(-1))
    kv = (g_own[0] + far_back[0] + near_back.astype(F32) + last_back.astype(F32)).astype(BF16)

    dqs = [dq] + [lax.ppermute(dq, "head", head_shift(-2 * r)) for r in (1, 2, 3)]
    acc = call(
        proj_q_kernel, 0, dqs + [wq], sds((TILE, 1024), F32),
        flops=1_073_741_824, nbytes=6_000_000,
    )
    kvs = [kv] + [lax.ppermute(kv, "head", head_shift(-2 * r)) for r in (1, 2, 3)]
    send, keep = call(
        proj_kv_kernel, 0, kvs + [wkv, acc],
        (sds((TILE, 512), BF16), sds((TILE, 512), F32)),
        flops=536_870_912, nbytes=4_000_000,
    )
    got = lax.ppermute(send, "head", HEAD_PAIR)
    return (keep + got.astype(F32)).astype(BF16)


def solution(mesh):
    placed = (
        P("ctx", "head"),
        P("ctx", "head"),
        P("ctx", "head"),
        P("ctx", "head"),
        P("ctx", "head"),
        P(),
        P("ctx", "head", None),
    )
    return jax.shard_map(
        shards, mesh=mesh, in_specs=placed, out_specs=P("ctx", "head"), check_vma=False
    )
```

```python
import jax
import jax.numpy as jnp
from jax import lax
from jax.experimental import pallas as pl
from jax.experimental.pallas import tpu as pltpu
from jax.sharding import PartitionSpec as P


HD = 128
GROUP = 4
TILE = 256
NX = 4
NZ = 8
NCHIP = NX * NZ
NHEAD = 8
SLOTS = 8
DOCS = 64
LOG2E = 1.4426950408889634
SCALE = HD ** (-0.5)
F32 = jnp.float32
BF16 = jnp.bfloat16


def ctx_of(x, z, c):
    return 2 * (NZ * (x % NX) + z % NZ) + c


def chip_shift(by):
    return [(2 * q + c, 2 * ((q + by) % NCHIP) + c) for q in range(NCHIP) for c in range(2)]


Z_RINGS = [[ctx_of(x, z, c) for z in range(NZ)] for x in range(NX) for c in range(2)]
X_SPLIT = [
    (ctx_of(x, z, c), ctx_of(x + 1 - 2 * c, z, c))
    for x in range(NX) for z in range(NZ) for c in range(2)
]
CORE_SWAP = [(d, d ^ 1) for d in range(2 * NCHIP)]
CORES = [[2 * q, 2 * q + 1] for q in range(NCHIP)]
LAST_TILE = [(2 * q, 2 * q + 1) for q in range(NCHIP)] + [
    (2 * q + 1, 2 * ((q + 4) % NCHIP)) for q in range(NCHIP)
]
LAST_TILE_BACK = [(b, a) for a, b in LAST_TILE]


WEIGHT_TRANSPOSE = [
    (ctx_of(x, z, c) * NHEAD + 2 * a + b, ctx_of(a, z, c) * NHEAD + 2 * x + b)
    for x in range(NX) for z in range(NZ) for c in range(2)
    for a in range(NX) for b in range(2)
]


def head_shift(by):
    return [(j, (j + by) % NHEAD) for j in range(NHEAD)]


SAME_PARITY = [[b + 2 * a for a in range(4)] for b in range(2)]
HEAD_PAIRS = [[2 * k, 2 * k + 1] for k in range(4)]

NT = (((1,), (1,)), ((), ()))
NN = (((1,), (0,)), ((), ()))
TN = (((0,), (0,)), ((), ()))


def dot(a, b, dims):
    return lax.dot_general(a, b, dims, preferred_element_type=F32)


def attention_kernel(
    me, lengths, q_ref, do_ref, out_ref, own, last, o1, o23, both,
    dq_ref, g_own, g_last, g_x, scores,
):
    i = me[0]
    chip, core = i // 2, i % 2
    other = 1 - core
    q_pos = i * TILE + lax.broadcasted_iota(jnp.int32, (1, TILE), 1)
    start = jnp.zeros((1, TILE), jnp.int32)
    end = jnp.int32(0)
    for d in range(DOCS):
        end = end + lengths[d]
        start = jnp.where(end <= q_pos, end, start)
    q_all = jnp.concatenate([q_ref[:, h * HD:(h + 1) * HD] for h in range(GROUP)], axis=0)
    do_all = jnp.concatenate([do_ref[:, h * HD:(h + 1) * HD] for h in range(GROUP)], axis=0)
    out_all = jnp.concatenate([out_ref[:, h * HD:(h + 1) * HD] for h in range(GROUP)], axis=0)
    prod = do_all.astype(F32) * out_all.astype(F32)
    high = prod.astype(BF16)
    low = (prod - high.astype(F32)).astype(BF16)
    ones = jnp.ones((16, HD), BF16)
    delta = (dot(ones, high, NT) + dot(ones, low, NT))[0:1, :]
    row = lax.broadcasted_iota(jnp.int32, (TILE, TILE), 0)
    last_tile = jnp.where(core == 1, 2 * chip, 2 * chip - 7)
    tiles = [
        (own, i), (o1, 2 * (chip - 1) + core), (o23.at[0], 2 * (chip - 2) + core),
        (o23.at[1], 2 * (chip - 3) + core), (last, last_tile),
    ] + [(both.at[other, n], 2 * (chip - 1 - n) + other) for n in range(3)]
    width = GROUP * TILE
    top = jnp.full((8, width), -1e30, F32)
    for t, (tile, number) in enumerate(tiles):
        raw = dot(tile[0], q_all, NT)
        k_pos = number * TILE + row
        allowed = (k_pos >= start) & (k_pos <= q_pos)
        parts = []
        for h in range(GROUP):
            part = jnp.where(allowed, raw[:, h * TILE:(h + 1) * TILE], -1e30)
            scores[pl.ds(t * TILE, TILE), pl.ds(h * TILE, TILE)] = part
            parts.append(jnp.max(part.reshape(TILE // 8, 8, TILE), axis=0))
        top = jnp.maximum(top, jnp.concatenate(parts, axis=1))
    top = jnp.max(top, axis=0, keepdims=True)
    total = jnp.zeros((8, width), F32)
    for t in range(SLOTS):
        e = jnp.exp2((scores[pl.ds(t * TILE, TILE), :] - top) * (SCALE * LOG2E))
        scores[pl.ds(t * TILE, TILE), :] = e
        total = total + jnp.sum(e.reshape(TILE // 8, 8, width), axis=0)
    total = jnp.sum(total, axis=0, keepdims=True)
    inv = 1.0 / total
    dq = [jnp.zeros((TILE, HD), F32) for _ in range(GROUP)]
    for t, (tile, _) in enumerate(tiles):
        probs = scores[pl.ds(t * TILE, TILE), :] * inv
        dprobs = dot(tile[1], do_all, NT)
        dscore = (probs * (dprobs - delta) * SCALE).astype(BF16)
        dv = dot(probs.astype(BF16), do_all, NN)
        dk = dot(dscore, q_all, NN)
        for h in range(GROUP):
            dq[h] = dq[h] + dot(dscore[:, h * TILE:(h + 1) * TILE], tile[0], TN)
        if t < 4:
            g_own[t, 0] = dk
            g_own[t, 1] = dv
        elif t == 4:
            g_last[0] = dk.astype(BF16)
            g_last[1] = dv.astype(BF16)
        else:
            g_x[t - 5, 0] = dk.astype(BF16)
            g_x[t - 5, 1] = dv.astype(BF16)
    for h in range(GROUP):
        dq_ref[:, h * HD:(h + 1) * HD] = dq[h].astype(BF16)


def project(me, heads, blocks, cols, acc_ref):
    x, core = me[1], me[3]
    up = 1 - 2 * core
    own, near, other, half, rest = blocks
    first, second = slice(0, 512), slice(512, 1024)
    here, behind, ahead = heads[x], heads[(x - up + NX) % NX], heads[(x + up + NX) % NX]
    far = heads[(x + 2) % NX]
    for side, rows, swapped, last in ((0, first, second, half), (1, second, first, rest)):
        acc_ref[side] = (
            acc_ref[side] + dot(here, own[rows, cols], NT) + dot(behind, near[rows, cols], NT)
            + dot(ahead, other[swapped, cols], NT) + dot(far, last[:, cols], NT)
        )


def proj_q_kernel(me, d0, d1, d2, d3, *refs):
    blocks, (acc_ref, heads) = refs[:5], refs[5:]
    for r, d in enumerate((d0, d1, d2, d3)):
        heads[(me[4] + r) % NX] = d[...]
    acc_ref[...] = jnp.zeros_like(acc_ref)
    project(me, heads, blocks, slice(0, 512), acc_ref)


def proj_kv_kernel(me, kv_ref, acc_in, *refs):
    blocks, (send_ref, keep_ref, heads, acc_ref, full) = refs[:5], refs[5:]
    core, b = me[3], me[5]
    for a in range(NX):
        heads[a, :, :HD] = kv_ref[a, 0]
        heads[a, :, HD:] = kv_ref[a, 1]
    acc_ref[...] = acc_in[...]
    project(me, heads, blocks, slice(512, 768), acc_ref)
    left = lax.broadcasted_iota(jnp.int32, (TILE, 128), 1) < 64
    for n in range(4):
        lanes = slice(128 * n, 128 * n + 128)
        even, odd = acc_ref[core, :, lanes], acc_ref[1 - core, :, lanes]
        at = (n % 2) * 256
        full[n // 2, :, at:at + 128] = jnp.where(left, even, pltpu.roll(odd, 64, 1))
        full[n // 2, :, at + 128:at + 256] = jnp.where(left, pltpu.roll(even, 64, 1), odd)
    send_ref[...] = full[1 - b].astype(BF16)
    keep_ref[...] = full[b]


def call(kernel, n_scalar, args, outs, scratch=(), flops=0, nbytes=0, mib=8):
    vmem = pl.BlockSpec(memory_space=pltpu.VMEM)
    smem = pl.BlockSpec(memory_space=pltpu.SMEM)
    return pl.pallas_call(
        kernel,
        out_shape=outs,
        in_specs=[smem] * n_scalar + [vmem] * (len(args) - n_scalar),
        out_specs=jax.tree.map(lambda _: vmem, outs),
        scratch_shapes=list(scratch),
        cost_estimate=pl.CostEstimate(flops=flops, bytes_accessed=nbytes, transcendentals=0),
        compiler_params=pltpu.CompilerParams(vmem_limit_bytes=mib * 1024 * 1024),
    )(*args)


def sds(shape, dtype):
    return jax.ShapeDtypeStruct(shape, dtype)


def gather(array, axis, groups):
    return lax.all_gather(array, axis, axis=0, axis_index_groups=groups)


def step(queries, keys, values, out_grad, attn_out, lengths, proj_weight):
    i = lax.axis_index("ctx")
    j = lax.axis_index("head")
    chip, core = i // 2, i % 2
    k, b = j // 2, j % 2
    me = jnp.stack([i, chip // NZ, chip % NZ, core, k, b]).astype(jnp.int32)

    own = jnp.stack([keys, values])
    o1 = lax.ppermute(own, "ctx", chip_shift(1))
    last = lax.ppermute(own, "ctx", LAST_TILE)
    o23 = lax.ppermute(jnp.stack([own, o1]), "ctx", chip_shift(2))
    both = gather(jnp.concatenate([o1[None], o23]), "ctx", CORES)

    w = lax.ppermute(proj_weight.reshape(64, 768), ("ctx", "head"), WEIGHT_TRANSPOSE)
    w = gather(w, "ctx", Z_RINGS).reshape(512, 768)
    w = jnp.concatenate([w, lax.ppermute(w, "ctx", CORE_SWAP)])
    w1 = lax.ppermute(w, "ctx", X_SPLIT)
    w2 = lax.ppermute(w1[:512], "ctx", X_SPLIT)
    weights = [w, w1, lax.ppermute(w1, "ctx", CORE_SWAP), w2, lax.ppermute(w2, "ctx", CORE_SWAP)]

    dq, g_own, g_last, g_x = call(
        attention_kernel, 2,
        [me, lengths, queries, out_grad, attn_out, own, last, o1, o23, both],
        (
            sds((TILE, GROUP * HD), BF16),
            sds((4, 2, TILE, HD), F32),
            sds((2, TILE, HD), BF16),
            sds((3, 2, TILE, HD), BF16),
        ),
        scratch=[pltpu.VMEM((SLOTS * TILE, GROUP * TILE), F32)],
        flops=2_700_000_000, nbytes=5_000_000, mib=18,
    )

    swapped = gather(g_x, "ctx", CORES)
    x_back = lax.dynamic_index_in_dim(swapped, 1 - core, 0, keepdims=False)
    far = (g_own[2:] + x_back[1:].astype(F32)).astype(BF16)
    far_back = lax.ppermute(far, "ctx", chip_shift(-2))
    last_back = lax.ppermute(g_last, "ctx", LAST_TILE_BACK)
    near = (g_own[1] + x_back[0].astype(F32) + far_back[1].astype(F32)).astype(BF16)
    near_back = lax.ppermute(near, "ctx", chip_shift(-1))
    kv = (
        g_own[0] + far_back[0].astype(F32) + near_back.astype(F32) + last_back.astype(F32)
    ).astype(BF16)

    dqs = [dq] + [lax.ppermute(dq, "head", head_shift(-2 * r)) for r in (1, 2, 3)]
    acc = call(
        proj_q_kernel, 1, [me] + dqs + weights, sds((2, TILE, 512), F32),
        scratch=[pltpu.VMEM((NX, TILE, 512), BF16)],
        flops=1_073_741_824, nbytes=6_000_000,
    )
    kvs = gather(kv, "head", SAME_PARITY)
    send, keep = call(
        proj_kv_kernel, 1, [me, kvs, acc] + weights,
        (sds((TILE, 512), BF16), sds((TILE, 512), F32)),
        scratch=[pltpu.VMEM((NX, TILE, 256), BF16)] + [pltpu.VMEM((2, TILE, 512), F32)] * 2,
        flops=536_870_912, nbytes=4_000_000,
    )
    got = gather(send, "head", HEAD_PAIRS)
    got = lax.dynamic_index_in_dim(got, 1 - b, 0, keepdims=False)
    return (keep + got.astype(F32)).astype(BF16)


def solution(mesh):
    placed = (
        P("ctx", "head"),
        P("ctx", "head"),
        P("ctx", "head"),
        P("ctx", "head"),
        P("ctx", "head"),
        P(),
        P("ctx", "head", None),
    )
    return jax.shard_map(
        step, mesh=mesh, in_specs=placed, out_specs=P("ctx", "head"), check_vma=False
    )
```

```python
import jax
import jax.numpy as jnp
from jax import lax
from jax.experimental import pallas as pl
from jax.experimental.pallas import tpu as pltpu
from jax.sharding import PartitionSpec as P


HD = 128
GROUP = 4
TILE = 256
NX = 4
NZ = 8
NCHIP = NX * NZ
NHEAD = 8
SLOTS = 8
Z_ORDER = (0, 2, 4, 6, 7, 1, 3, 5)
DOCS = 64
LOG2E = 1.4426950408889634
SCALE = HD ** (-0.5)
F32 = jnp.float32
BF16 = jnp.bfloat16


def ctx_of(x, z, c):
    return 2 * (NZ * (x % NX) + z % NZ) + c


def chip_shift(by):
    return [(2 * q + c, 2 * ((q + by) % NCHIP) + c) for q in range(NCHIP) for c in range(2)]


def z_shift(by):
    return [
        (ctx_of(x, z, c), ctx_of(x, z + by, c))
        for x in range(NX) for z in range(NZ) for c in range(2)
    ]


X_SPLIT = [
    (ctx_of(x, z, c), ctx_of(x + 1 - 2 * c, z, c))
    for x in range(NX) for z in range(NZ) for c in range(2)
]
CORE_SWAP = [(d, d ^ 1) for d in range(2 * NCHIP)]
CORES = [[2 * q, 2 * q + 1] for q in range(NCHIP)]
LAST_TILE = [(2 * q, 2 * q + 1) for q in range(NCHIP)] + [
    (2 * q + 1, 2 * ((q + 4) % NCHIP)) for q in range(NCHIP)
]
LAST_TILE_BACK = [(b, a) for a, b in LAST_TILE]


WEIGHT_TRANSPOSE = [
    (ctx_of(x, z, c) * NHEAD + 2 * a + b, ctx_of(a, z, c) * NHEAD + 2 * x + b)
    for x in range(NX) for z in range(NZ) for c in range(2)
    for a in range(NX) for b in range(2)
]


def head_shift(by):
    return [(j, (j + by) % NHEAD) for j in range(NHEAD)]


HEAD_PAIRS = [[2 * k, 2 * k + 1] for k in range(4)]

NT = (((1,), (1,)), ((), ()))
NN = (((1,), (0,)), ((), ()))
TN = (((0,), (0,)), ((), ()))


def dot(a, b, dims):
    return lax.dot_general(a, b, dims, preferred_element_type=F32)


def attention_kernel(
    me, lengths, q_ref, do_ref, out_ref, own, last, o1, o23, both,
    dq_ref, g_own, g_last, g_x, scores,
):
    i = me[0]
    chip, core = i // 2, i % 2
    other = 1 - core
    q_pos = i * TILE + lax.broadcasted_iota(jnp.int32, (1, TILE), 1)
    start = jnp.zeros((1, TILE), jnp.int32)
    end = jnp.int32(0)
    for d in range(DOCS):
        end = end + lengths[d]
        start = jnp.where(end <= q_pos, end, start)
    q_all = jnp.concatenate([q_ref[:, h * HD:(h + 1) * HD] for h in range(GROUP)], axis=0)
    do_all = jnp.concatenate([do_ref[:, h * HD:(h + 1) * HD] for h in range(GROUP)], axis=0)
    out_all = jnp.concatenate([out_ref[:, h * HD:(h + 1) * HD] for h in range(GROUP)], axis=0)
    prod = do_all.astype(F32) * out_all.astype(F32)
    high = prod.astype(BF16)
    low = (prod - high.astype(F32)).astype(BF16)
    ones = jnp.ones((16, HD), BF16)
    delta = (dot(ones, high, NT) + dot(ones, low, NT))[0:1, :]
    row = lax.broadcasted_iota(jnp.int32, (TILE, TILE), 0)
    last_tile = jnp.where(core == 1, 2 * chip, 2 * chip - 7)
    tiles = [
        (own, i), (o1, 2 * (chip - 1) + core), (o23.at[0], 2 * (chip - 2) + core),
        (o23.at[1], 2 * (chip - 3) + core), (last, last_tile),
    ] + [(both.at[other, n], 2 * (chip - 1 - n) + other) for n in range(3)]
    width = GROUP * TILE
    top = jnp.full((8, width), -1e30, F32)
    for t, (tile, number) in enumerate(tiles):
        raw = dot(tile[0], q_all, NT)
        k_pos = number * TILE + row
        allowed = (k_pos >= start) & (k_pos <= q_pos)
        parts = []
        for h in range(GROUP):
            part = jnp.where(allowed, raw[:, h * TILE:(h + 1) * TILE], -1e30)
            scores[pl.ds(t * TILE, TILE), pl.ds(h * TILE, TILE)] = part
            parts.append(jnp.max(part.reshape(TILE // 8, 8, TILE), axis=0))
        top = jnp.maximum(top, jnp.concatenate(parts, axis=1))
    top = jnp.max(top, axis=0, keepdims=True)
    total = jnp.zeros((8, width), F32)
    for t in range(SLOTS):
        e = jnp.exp2((scores[pl.ds(t * TILE, TILE), :] - top) * (SCALE * LOG2E))
        scores[pl.ds(t * TILE, TILE), :] = e
        total = total + jnp.sum(e.reshape(TILE // 8, 8, width), axis=0)
    total = jnp.sum(total, axis=0, keepdims=True)
    inv = 1.0 / total
    dq = [jnp.zeros((TILE, HD), F32) for _ in range(GROUP)]
    for t, (tile, _) in enumerate(tiles):
        probs = scores[pl.ds(t * TILE, TILE), :] * inv
        dprobs = dot(tile[1], do_all, NT)
        dscore = (probs * (dprobs - delta) * SCALE).astype(BF16)
        dv = dot(probs.astype(BF16), do_all, NN)
        dk = dot(dscore, q_all, NN)
        for h in range(GROUP):
            dq[h] = dq[h] + dot(dscore[:, h * TILE:(h + 1) * TILE], tile[0], TN)
        if t < 4:
            g_own[t, 0] = dk
            g_own[t, 1] = dv
        elif t == 4:
            g_last[0] = dk.astype(BF16)
            g_last[1] = dv.astype(BF16)
        else:
            g_x[t - 5, 0] = dk.astype(BF16)
            g_x[t - 5, 1] = dv.astype(BF16)
    for h in range(GROUP):
        dq_ref[:, h * HD:(h + 1) * HD] = dq[h].astype(BF16)


FIRST, SECOND = slice(0, 512), slice(512, 1024)


def proj_kernel(
    me, d0, d1, d2, d3, k0, k1, k2, k3, own, near, other, last,
    send_ref, keep_ref, heads, acc_ref, full,
):
    x, core, k, b = me[1], me[3], me[4], me[5]
    for r, (d, kv) in enumerate(((d0, k0), (d1, k1), (d2, k2), (d3, k3))):
        a = (k + r) % NX
        heads[a, :, :512] = d[...]
        heads[a, :, 512:640] = kv[0]
        heads[a, :, 640:] = kv[1]
    up = 1 - 2 * core
    here, behind, ahead = heads[x], heads[(x - up + NX) % NX], heads[(x + up + NX) % NX]
    far = heads[(x + 2) % NX]
    for side, rows, swapped in ((0, FIRST, SECOND), (1, SECOND, FIRST)):
        acc_ref[side] = (
            dot(here, own[rows, :], NT) + dot(behind, near[rows, :], NT)
            + dot(ahead, other[swapped, :], NT) + dot(far, last[rows, :], NT)
        )
    left = lax.broadcasted_iota(jnp.int32, (TILE, 128), 1) < 64
    for n in range(4):
        lanes = slice(128 * n, 128 * n + 128)
        even, odd = acc_ref[core, :, lanes], acc_ref[1 - core, :, lanes]
        at = (n % 2) * 256
        full[n // 2, :, at:at + 128] = jnp.where(left, even, pltpu.roll(odd, 64, 1))
        full[n // 2, :, at + 128:at + 256] = jnp.where(left, pltpu.roll(even, 64, 1), odd)
    send_ref[...] = full[1 - b].astype(BF16)
    keep_ref[...] = full[b]


def call(kernel, n_scalar, args, outs, scratch=(), flops=0, nbytes=0, mib=6):
    vmem = pl.BlockSpec(memory_space=pltpu.VMEM)
    smem = pl.BlockSpec(memory_space=pltpu.SMEM)
    return pl.pallas_call(
        kernel,
        out_shape=outs,
        in_specs=[smem] * n_scalar + [vmem] * (len(args) - n_scalar),
        out_specs=jax.tree.map(lambda _: vmem, outs),
        scratch_shapes=list(scratch),
        cost_estimate=pl.CostEstimate(flops=flops, bytes_accessed=nbytes, transcendentals=0),
        compiler_params=pltpu.CompilerParams(vmem_limit_bytes=mib * 1024 * 1024),
    )(*args)


def sds(shape, dtype):
    return jax.ShapeDtypeStruct(shape, dtype)


def gather(array, axis, groups):
    return lax.all_gather(array, axis, axis=0, axis_index_groups=groups)


def in_order(w, z):
    out = w
    for slot, dz in enumerate(Z_ORDER):
        piece = w[64 * slot:64 * slot + 64]
        out = lax.dynamic_update_slice_in_dim(out, piece, (z + dz) % NZ * 64, 0)
    return out


def step(queries, keys, values, out_grad, attn_out, lengths, proj_weight):
    i = lax.axis_index("ctx")
    j = lax.axis_index("head")
    chip, core = i // 2, i % 2
    k, b = j // 2, j % 2
    me = jnp.stack([i, chip // NZ, chip % NZ, core, k, b]).astype(jnp.int32)

    own = jnp.stack([keys, values])
    o1 = lax.ppermute(own, "ctx", chip_shift(1))
    last = lax.ppermute(own, "ctx", LAST_TILE)
    o23 = lax.ppermute(jnp.stack([own, o1]), "ctx", chip_shift(2))
    both = gather(jnp.concatenate([o1[None], o23]), "ctx", CORES)

    w = lax.ppermute(proj_weight.reshape(64, 768), ("ctx", "head"), WEIGHT_TRANSPOSE)
    for by in (-2, -4, 1):
        w = jnp.concatenate([w, lax.ppermute(w, "ctx", z_shift(by))])
    w = in_order(w, chip % NZ)
    w = jnp.concatenate([w, lax.ppermute(w, "ctx", CORE_SWAP)])
    w1 = lax.ppermute(w, "ctx", X_SPLIT)
    w2 = lax.ppermute(w1, "ctx", X_SPLIT)
    weights = [w, w1, lax.ppermute(w1, "ctx", CORE_SWAP), w2]

    dq, g_own, g_last, g_x = call(
        attention_kernel, 2,
        [me, lengths, queries, out_grad, attn_out, own, last, o1, o23, both],
        (
            sds((TILE, GROUP * HD), BF16),
            sds((4, 2, TILE, HD), F32),
            sds((2, TILE, HD), BF16),
            sds((3, 2, TILE, HD), BF16),
        ),
        scratch=[pltpu.VMEM((SLOTS * TILE, GROUP * TILE), F32)],
        flops=2_700_000_000, nbytes=5_000_000, mib=10,
    )

    swapped = gather(g_x, "ctx", CORES)
    x_back = lax.dynamic_index_in_dim(swapped, 1 - core, 0, keepdims=False)
    far = (g_own[2:] + x_back[1:].astype(F32)).astype(BF16)
    far_back = lax.ppermute(far, "ctx", chip_shift(-2))
    last_back = lax.ppermute(g_last, "ctx", LAST_TILE_BACK)
    near = (g_own[1] + x_back[0].astype(F32) + far_back[1].astype(F32)).astype(BF16)
    near_back = lax.ppermute(near, "ctx", chip_shift(-1))
    kv = (
        g_own[0] + far_back[0].astype(F32) + near_back.astype(F32) + last_back.astype(F32)
    ).astype(BF16)

    dqs = [dq] + [lax.ppermute(dq, "head", head_shift(-2 * r)) for r in (1, 2, 3)]
    kvs = [kv] + [lax.ppermute(kv, "head", head_shift(-2 * r)) for r in (1, 2, 3)]
    send, keep = call(
        proj_kernel, 1, [me] + dqs + kvs + weights,
        (sds((TILE, 512), BF16), sds((TILE, 512), F32)),
        scratch=[
            pltpu.VMEM((NX, TILE, 768), BF16), pltpu.VMEM((2, TILE, 512), F32),
            pltpu.VMEM((2, TILE, 512), F32),
        ],
        flops=1_610_612_736, nbytes=8_000_000, mib=16,
    )
    got = gather(send, "head", HEAD_PAIRS)
    got = lax.dynamic_index_in_dim(got, 1 - b, 0, keepdims=False)
    return (keep + got.astype(F32)).astype(BF16)


def solution(mesh):
    placed = (
        P("ctx", "head"),
        P("ctx", "head"),
        P("ctx", "head"),
        P("ctx", "head"),
        P("ctx", "head"),
        P(),
        P("ctx", "head", None),
    )
    return jax.shard_map(
        step, mesh=mesh, in_specs=placed, out_specs=P("ctx", "head"), check_vma=False
    )
```

```python
import jax
import jax.numpy as jnp
from jax import lax
from jax.experimental import pallas as pl
from jax.experimental.pallas import tpu as pltpu
from jax.sharding import PartitionSpec as P


HD = 128
GROUP = 4
TILE = 256
NX = 4
NZ = 8
NCHIP = NX * NZ
NHEAD = 8
SLOTS = 8
Z_ORDER = (0, 2, 4, 6, 7, 1, 3, 5)
DOCS = 64
LOG2E = 1.4426950408889634
SCALE = HD ** (-0.5)
F32 = jnp.float32
BF16 = jnp.bfloat16


def ctx_of(x, z, c):
    return 2 * (NZ * (x % NX) + z % NZ) + c


def chip_shift(by):
    return [(2 * q + c, 2 * ((q + by) % NCHIP) + c) for q in range(NCHIP) for c in range(2)]


def z_shift(by):
    return [
        (ctx_of(x, z, c), ctx_of(x, z + by, c))
        for x in range(NX) for z in range(NZ) for c in range(2)
    ]


X_SPLIT = [
    (ctx_of(x, z, c), ctx_of(x + 1 - 2 * c, z, c))
    for x in range(NX) for z in range(NZ) for c in range(2)
]
CORE_SWAP = [(d, d ^ 1) for d in range(2 * NCHIP)]
CORES = [[2 * q, 2 * q + 1] for q in range(NCHIP)]
LAST_TILE = [(2 * q, 2 * q + 1) for q in range(NCHIP)] + [
    (2 * q + 1, 2 * ((q + 4) % NCHIP)) for q in range(NCHIP)
]
LAST_TILE_BACK = [(b, a) for a, b in LAST_TILE]


WEIGHT_TRANSPOSE = [
    (ctx_of(x, z, c) * NHEAD + 2 * a + b, ctx_of(a, z, c) * NHEAD + 2 * x + b)
    for x in range(NX) for z in range(NZ) for c in range(2)
    for a in range(NX) for b in range(2)
]


def head_shift(by):
    return [(j, (j + by) % NHEAD) for j in range(NHEAD)]


HEAD_PAIRS = [[2 * k, 2 * k + 1] for k in range(4)]

NT = (((1,), (1,)), ((), ()))
NN = (((1,), (0,)), ((), ()))
TN = (((0,), (0,)), ((), ()))


def dot(a, b, dims):
    return lax.dot_general(a, b, dims, preferred_element_type=F32)


def attention_kernel(
    me, lengths, q_ref, do_ref, out_ref, own, last, o1, o23, both,
    dq_ref, g_own, g_last, g_x, scores,
):
    i = me[0]
    chip, core = i // 2, i % 2
    other = 1 - core
    q_pos = i * TILE + lax.broadcasted_iota(jnp.int32, (1, TILE), 1)
    start = jnp.zeros((1, TILE), jnp.int32)
    end = jnp.int32(0)
    for d in range(DOCS):
        end = end + lengths[d]
        start = jnp.where(end <= q_pos, end, start)
    q_all = jnp.concatenate([q_ref[:, h * HD:(h + 1) * HD] for h in range(GROUP)], axis=0)
    do_all = jnp.concatenate([do_ref[:, h * HD:(h + 1) * HD] for h in range(GROUP)], axis=0)
    out_all = jnp.concatenate([out_ref[:, h * HD:(h + 1) * HD] for h in range(GROUP)], axis=0)
    prod = do_all.astype(F32) * out_all.astype(F32)
    high = prod.astype(BF16)
    low = (prod - high.astype(F32)).astype(BF16)
    ones = jnp.ones((16, HD), BF16)
    delta = (dot(ones, high, NT) + dot(ones, low, NT))[0:1, :]
    row = lax.broadcasted_iota(jnp.int32, (TILE, TILE), 0)
    last_tile = jnp.where(core == 1, 2 * chip, 2 * chip - 7)
    tiles = [
        (own, i), (o1, 2 * (chip - 1) + core), (o23.at[0], 2 * (chip - 2) + core),
        (o23.at[1], 2 * (chip - 3) + core), (last, last_tile),
    ] + [(both.at[other, n], 2 * (chip - 1 - n) + other) for n in range(3)]
    width = GROUP * TILE
    top = jnp.full((8, width), -1e30, F32)
    for t, (tile, number) in enumerate(tiles):
        raw = dot(tile[0], q_all, NT)
        k_pos = number * TILE + row
        allowed = (k_pos >= start) & (k_pos <= q_pos)
        parts = []
        for h in range(GROUP):
            part = jnp.where(allowed, raw[:, h * TILE:(h + 1) * TILE], -1e30)
            scores[pl.ds(t * TILE, TILE), pl.ds(h * TILE, TILE)] = part
            parts.append(jnp.max(part.reshape(TILE // 8, 8, TILE), axis=0))
        top = jnp.maximum(top, jnp.concatenate(parts, axis=1))
    top = jnp.max(top, axis=0, keepdims=True)
    total = jnp.zeros((8, width), F32)
    for t in range(SLOTS):
        e = jnp.exp2((scores[pl.ds(t * TILE, TILE), :] - top) * (SCALE * LOG2E))
        scores[pl.ds(t * TILE, TILE), :] = e
        total = total + jnp.sum(e.reshape(TILE // 8, 8, width), axis=0)
    total = jnp.sum(total, axis=0, keepdims=True)
    inv = 1.0 / total
    dq = [jnp.zeros((TILE, HD), F32) for _ in range(GROUP)]
    for t, (tile, _) in enumerate(tiles):
        probs = scores[pl.ds(t * TILE, TILE), :] * inv
        dprobs = dot(tile[1], do_all, NT)
        dscore = (probs * (dprobs - delta) * SCALE).astype(BF16)
        dv = dot(probs.astype(BF16), do_all, NN)
        dk = dot(dscore, q_all, NN)
        for h in range(GROUP):
            dq[h] = dq[h] + dot(dscore[:, h * TILE:(h + 1) * TILE], tile[0], TN)
        if t < 4:
            g_own[t, 0] = dk
            g_own[t, 1] = dv
        elif t == 4:
            g_last[0] = dk.astype(BF16)
            g_last[1] = dv.astype(BF16)
        else:
            g_x[t - 5, 0] = dk.astype(BF16)
            g_x[t - 5, 1] = dv.astype(BF16)
    for h in range(GROUP):
        dq_ref[:, h * HD:(h + 1) * HD] = dq[h].astype(BF16)


FIRST, SECOND = slice(0, 512), slice(512, 1024)


def proj_kernel(
    me, d0, d1, d2, d3, k0, k1, k2, k3, own, near, other, half, rest,
    send_ref, keep_ref, heads, acc_ref, full,
):
    x, core, k, b = me[1], me[3], me[4], me[5]
    for r, (d, kv) in enumerate(((d0, k0), (d1, k1), (d2, k2), (d3, k3))):
        a = (k + r) % NX
        heads[a, :, :512] = d[...]
        heads[a, :, 512:640] = kv[0]
        heads[a, :, 640:] = kv[1]
    up = 1 - 2 * core
    here, behind, ahead = heads[x], heads[(x - up + NX) % NX], heads[(x + up + NX) % NX]
    far = heads[(x + 2) % NX]
    for side, rows, swapped, last in ((0, FIRST, SECOND, half), (1, SECOND, FIRST, rest)):
        acc_ref[side] = (
            dot(here, own[rows, :], NT) + dot(behind, near[rows, :], NT)
            + dot(ahead, other[swapped, :], NT) + dot(far, last[...], NT)
        )
    left = lax.broadcasted_iota(jnp.int32, (TILE, 128), 1) < 64
    for n in range(4):
        lanes = slice(128 * n, 128 * n + 128)
        even, odd = acc_ref[core, :, lanes], acc_ref[1 - core, :, lanes]
        at = (n % 2) * 256
        full[n // 2, :, at:at + 128] = jnp.where(left, even, pltpu.roll(odd, 64, 1))
        full[n // 2, :, at + 128:at + 256] = jnp.where(left, pltpu.roll(even, 64, 1), odd)
    send_ref[...] = full[1 - b].astype(BF16)
    keep_ref[...] = full[b]


def call(kernel, n_scalar, args, outs, scratch=(), flops=0, nbytes=0, mib=6):
    vmem = pl.BlockSpec(memory_space=pltpu.VMEM)
    smem = pl.BlockSpec(memory_space=pltpu.SMEM)
    return pl.pallas_call(
        kernel,
        out_shape=outs,
        in_specs=[smem] * n_scalar + [vmem] * (len(args) - n_scalar),
        out_specs=jax.tree.map(lambda _: vmem, outs),
        scratch_shapes=list(scratch),
        cost_estimate=pl.CostEstimate(flops=flops, bytes_accessed=nbytes, transcendentals=0),
        compiler_params=pltpu.CompilerParams(vmem_limit_bytes=mib * 1024 * 1024),
    )(*args)


def sds(shape, dtype):
    return jax.ShapeDtypeStruct(shape, dtype)


def gather(array, axis, groups):
    return lax.all_gather(array, axis, axis=0, axis_index_groups=groups)


def in_order(w, z):
    out = w
    for slot, dz in enumerate(Z_ORDER):
        piece = w[64 * slot:64 * slot + 64]
        out = lax.dynamic_update_slice_in_dim(out, piece, (z + dz) % NZ * 64, 0)
    return out


def step(queries, keys, values, out_grad, attn_out, lengths, proj_weight):
    i = lax.axis_index("ctx")
    j = lax.axis_index("head")
    chip, core = i // 2, i % 2
    k, b = j // 2, j % 2
    me = jnp.stack([i, chip // NZ, chip % NZ, core, k, b]).astype(jnp.int32)

    own = jnp.stack([keys, values])
    o1 = lax.ppermute(own, "ctx", chip_shift(1))
    last = lax.ppermute(own, "ctx", LAST_TILE)
    o23 = lax.ppermute(jnp.stack([own, o1]), "ctx", chip_shift(2))
    both = gather(jnp.concatenate([o1[None], o23]), "ctx", CORES)

    w = lax.ppermute(proj_weight.reshape(64, 768), ("ctx", "head"), WEIGHT_TRANSPOSE)
    for by in (-2, -4, 1):
        w = jnp.concatenate([w, lax.ppermute(w, "ctx", z_shift(by))])
    w = in_order(w, chip % NZ)
    w = jnp.concatenate([w, lax.ppermute(w, "ctx", CORE_SWAP)])
    w1 = lax.ppermute(w, "ctx", X_SPLIT)
    w2 = lax.ppermute(w1[:512], "ctx", X_SPLIT)
    weights = [w, w1, lax.ppermute(w1, "ctx", CORE_SWAP), w2, lax.ppermute(w2, "ctx", CORE_SWAP)]

    dq, g_own, g_last, g_x = call(
        attention_kernel, 2,
        [me, lengths, queries, out_grad, attn_out, own, last, o1, o23, both],
        (
            sds((TILE, GROUP * HD), BF16),
            sds((4, 2, TILE, HD), F32),
            sds((2, TILE, HD), BF16),
            sds((3, 2, TILE, HD), BF16),
        ),
        scratch=[pltpu.VMEM((SLOTS * TILE, GROUP * TILE), F32)],
        flops=2_700_000_000, nbytes=5_000_000, mib=10,
    )

    swapped = gather(g_x, "ctx", CORES)
    x_back = lax.dynamic_index_in_dim(swapped, 1 - core, 0, keepdims=False)
    far = (g_own[2:] + x_back[1:].astype(F32)).astype(BF16)
    far_back = lax.ppermute(far, "ctx", chip_shift(-2))
    last_back = lax.ppermute(g_last, "ctx", LAST_TILE_BACK)
    near = (g_own[1] + x_back[0].astype(F32) + far_back[1].astype(F32)).astype(BF16)
    near_back = lax.ppermute(near, "ctx", chip_shift(-1))
    kv = (
        g_own[0] + far_back[0].astype(F32) + near_back.astype(F32) + last_back.astype(F32)
    ).astype(BF16)

    dqs = [dq] + [lax.ppermute(dq, "head", head_shift(-2 * r)) for r in (1, 2, 3)]
    kvs = [kv] + [lax.ppermute(kv, "head", head_shift(-2 * r)) for r in (1, 2, 3)]
    send, keep = call(
        proj_kernel, 1, [me] + dqs + kvs + weights,
        (sds((TILE, 512), BF16), sds((TILE, 512), F32)),
        scratch=[
            pltpu.VMEM((NX, TILE, 768), BF16), pltpu.VMEM((2, TILE, 512), F32),
            pltpu.VMEM((2, TILE, 512), F32),
        ],
        flops=1_610_612_736, nbytes=8_000_000, mib=16,
    )
    got = gather(send, "head", HEAD_PAIRS)
    got = lax.dynamic_index_in_dim(got, 1 - b, 0, keepdims=False)
    return (keep + got.astype(F32)).astype(BF16)


def solution(mesh):
    placed = (
        P("ctx", "head"),
        P("ctx", "head"),
        P("ctx", "head"),
        P("ctx", "head"),
        P("ctx", "head"),
        P(),
        P("ctx", "head", None),
    )
    return jax.shard_map(
        step, mesh=mesh, in_specs=placed, out_specs=P("ctx", "head"), check_vma=False
    )
```
